32 devices in a mesh: groups: 2 (over x), req: 16 (over z, y, core).
Axes of the slice: x: 2, y: 2, z: 4, core: 2. Of those that a mesh axis runs over, the one named last changes fastest.
Arguments:
- queries: bfloat16 [2, 2048, 512], P(None, ('groups', 'req')), parts along dimension 1, may hold values from -40 to 40
- new_kv: bfloat16 [2, 2048, 128], P(None, ('groups', 'req')), parts along dimension 1, may hold values from -4 to 4
- cache: bfloat16 [2, 2048, 128, 128], P(None, ('groups', 'req')), parts along dimension 1, may hold values from -4 to 4
- lengths: int32 [2, 256], P(None, 'groups'), parts along dimension 1, may hold values from 2 to 128
- residual: bfloat16 [2, 256, 2880], P(None, ('groups', 'req')), parts along dimension 1, may hold values from -30 to 30
- o_proj: bfloat16 [4096, 2880], P('req'), may hold values from -1 to 1
- router: bfloat16 [2880, 16], replicated, may hold values from -0.109375 to 0.109375
- w_gate: bfloat16 [64, 2880, 360], P('req'), may hold values from -0.109375 to 0.109375
- w_up: bfloat16 [64, 2880, 360], P('req'), may hold values from -0.109375 to 0.109375
- w_down: bfloat16 [64, 360, 2880], P('req'), may hold values from -0.15625 to 0.15625
- routes: int32 [2, 256, 4], P(None, ('groups', 'req')), parts along dimension 1, may hold values from 0 to 15, all different within a row; in each aligned block of 8 rows (0 to 7, 8 to 15, ..., all dimensions but the last counted through in order) at most 4 rows name the same one
Outputs:
- attended: bfloat16 [2, 256, 2880], P(None, ('groups', 'req')), parts along dimension 1
- layer_out: bfloat16 [2, 256, 2880], P(None, ('groups', 'req')), parts along dimension 1
The draws below stay inside these ranges and needn't reach their ends.
There are 2 independent parts, one for each index of `groups`. The reference program is written for one: setup_inputs(seed, part) draws one part's arguments, and reference() takes and returns one part's arrays. A program takes and returns all parts, laid end to end along the dimension named above; an argument that names none is the same for every part. Nothing has to cross between parts.
Inputs may be any that keep to these rules, and one draw needn't show every extreme that they name: `routes`: each row names 4 different experts; of the 8 rows of one device of one micro-batch at most 4 name any one expert, and in every draw some expert is named by exactly 4 rows of some device.
All inputs are finite; a program needn't handle non-finite values.
Results may differ from the reference program's by a relative error of at most 0.0075.
Values may be sent and summed in bfloat16 or wider, within the bound.
A program may use at most 128 MiB of HBM per device.

```python
import math
import jax
import jax.numpy as jnp
import numpy as np
from jax import lax

D = 2880
HD = 64
KVH = 8
QPK = 8
WIN = 128
EXPERTS = 16
FFW = 1440
SPLIT = 4
TOPK = 4
MB = 2
REQ_DEV = 8
FFS = 360
REQS = 128
CAP = 4


def draw_queries(key, part):
    shape_full = (MB, KVH * REQS, QPK * HD)
    values = jnp.clip(jax.random.normal(jax.random.fold_in(key, 1), shape_full, jnp.float32), -4.0, 4.0)
    return values.astype(jnp.bfloat16)


def draw_cache(key, part):
    shape_full = (MB, KVH * REQS, WIN, 2 * HD)
    values = jnp.clip(jax.random.normal(jax.random.fold_in(key, 2), shape_full, jnp.float32), -4.0, 4.0)
    return values.astype(jnp.bfloat16)


def draw_residual(key, part):
    shape_full = (MB, REQS, D)
    base = 0.5 * jnp.clip(jax.random.normal(jax.random.fold_in(key, 3), shape_full, jnp.float32), -3.0, 3.0)
    row_scale = jnp.exp(jax.random.uniform(jax.random.fold_in(key, 4), (MB, REQS, 1), jnp.float32, -1.15, 1.15))
    column_scale = jnp.exp(jax.random.uniform(jax.random.fold_in(key, 5), (1, 1, D), jnp.float32, -1.15, 1.15))
    return (base * row_scale * column_scale).astype(jnp.bfloat16)


def touch_ends(values, key, smallest, largest):
    place = [jax.random.randint(jax.random.fold_in(key, axis), (), 0, length) for axis, length in enumerate(values.shape)]
    main_axis = values.shape.index(max(values.shape))
    next_to = place[:main_axis] + [(place[main_axis] + 1) % values.shape[main_axis]] + place[main_axis + 1:]
    return values.at[tuple(place)].set(smallest).at[tuple(next_to)].set(largest)


def block_levels(rng, shape, pieces, low, largest):
    factor_of = 1.0
    for dim, shards_of in pieces:
        draws = jax.random.uniform(jax.random.fold_in(jax.random.fold_in(rng, 6), dim), (shards_of,), jnp.float32, low / len(pieces), largest / len(pieces))
        factor_of = factor_of * jnp.repeat(jnp.exp(draws), shape[dim] // shards_of).reshape((-1,) + (1,) * (len(shape) - 1 - dim))
    return factor_of


def deal_out(stream_key, own, number, rows, number_of, top, limit, skew):
    ranking = jax.random.permutation(stream_key, number_of)
    heavy_load, common = shares(number_of, rows * top, limit, skew, True), shares(number_of, rows * top, limit, skew, False)
    places = jnp.arange(number_of)

    def named(sizes, turn):
        used = int((sizes > 0).sum())
        fixed = max(1, used // 4)
        moved = fixed + (places - fixed + turn * (used - fixed)) % max(1, number_of - fixed)
        return jnp.zeros((number_of,), jnp.int32).at[ranking[jnp.where(places < fixed, places, moved)]].set(jnp.asarray(sizes, jnp.int32))

    sizes = jnp.where(number % 4 == 0, named(heavy_load, number // 4), named(common, number - number // 4 - 1))
    mixed = jax.random.permutation(jax.random.fold_in(own, 3), number_of)
    giver, receiver = mixed[0:number_of // 2 * 2:2], mixed[1:number_of // 2 * 2:2]
    slack = jnp.minimum(sizes[giver] - 1, limit - sizes[receiver]) // 2
    slack = jnp.where((giver == ranking[0]) | (receiver == ranking[0]) | (sizes[receiver] == 0), 0, jnp.maximum(slack, 0))
    moved = jax.random.randint(jax.random.fold_in(own, 4), (number_of // 2,), 0, 1 << 20) % (slack + 1)
    sizes = sizes.at[giver].add(-moved).at[receiver].add(moved)
    members = jnp.searchsorted(jnp.cumsum(sizes), jnp.arange(rows * top), side="right").astype(jnp.int32)
    grid = members.reshape(top, rows).T
    grid = grid[jax.random.permutation(jax.random.fold_in(own, 1), rows)]
    turn = jax.random.randint(jax.random.fold_in(own, 2), (rows, 1), 0, top)
    return jnp.take_along_axis(grid, (jnp.arange(top)[None, :] + turn) % top, axis=1)


def shares(number_of, total, most, lean, full):
    weights = [(1 << 20) // math.isqrt(grade ** lean) + 1 for grade in range(1, number_of + 1)]
    largest = most if full else min(most, max(-(-total // number_of), total * weights[0] // sum(weights)))
    least = 1 if total - largest >= number_of - 1 else 0
    given, spare = [largest] + [least] * (number_of - 1), total - largest - least * (number_of - 1)
    while spare > 0:
        movable = [i for i in range(1, number_of) if given[i] < largest] or [i for i in range(1, number_of) if given[i] < most]
        mass, remaining = sum([weights[i] for i in movable]), spare
        for i in movable:
            more = min(most - given[i], max(1, remaining * weights[i] // mass), spare)
            given[i] = given[i] + more
            spare = spare - more
    return np.array(given)


def bell_draw(own_key, dims, width, most, pieces=(), kind=jnp.bfloat16):
    values = jax.random.normal(own_key, dims, jnp.float32) * width
    if len(pieces) > 0:
        values = block_levels(own_key, dims, pieces, -0.22, 0.18) * values
    return jnp.clip(values, min=-most, max=most).astype(kind)


def setup_inputs(seed: int = 0, part: int = 0) -> dict:
    keys = jax.random.split(jax.random.key(seed), 12)
    part_splits = jax.random.split(jax.random.fold_in(keys[11], part), 12)
    queries = draw_queries(jax.random.fold_in(jax.random.fold_in(keys[11], part), 71), part)
    new_kv = bell_draw(part_splits[1], (MB, KVH * REQS, 2 * HD), 1.0, 4.0, ((1, 16),))
    cache = draw_cache(jax.random.fold_in(jax.random.fold_in(keys[11], part), 71), part)
    lengths = touch_ends(jax.random.randint(part_splits[3], (MB, REQS), 2, WIN + 1), jax.random.fold_in(part_splits[3], 1), 2, WIN).astype(jnp.int32)
    residual = draw_residual(jax.random.fold_in(jax.random.fold_in(keys[11], part), 71), part)
    o_proj = bell_draw(keys[5], (KVH * QPK * HD, D), 0.0625, 1.0, ((0, 16),))
    router = bell_draw(keys[6], (D, EXPERTS), D ** -0.5, 0.109375)
    w_gate = bell_draw(keys[7], (EXPERTS * SPLIT, D, FFS), D ** -0.5, 0.109375, ((0, 16),))
    w_up = bell_draw(keys[8], (EXPERTS * SPLIT, D, FFS), D ** -0.5, 0.109375, ((0, 16),))
    w_down = bell_draw(keys[9], (EXPERTS * SPLIT, FFS, D), FFW ** -0.5, 0.15625, ((0, 16),))
    routes_keys = jax.random.split(jax.random.fold_in(part_splits[10], 1), MB * REQS // REQ_DEV)
    routes_turns = jax.random.permutation(jax.random.fold_in(part_splits[10], 3), MB * REQS // REQ_DEV)
    routes = jax.vmap(lambda own, number: deal_out(jax.random.fold_in(part_splits[10], 2), own, number, REQ_DEV, EXPERTS, TOPK, CAP, 2))(routes_keys, routes_turns).reshape((MB, REQS, TOPK))
    return dict(queries=queries, new_kv=new_kv, cache=cache, lengths=lengths, residual=residual, o_proj=o_proj, router=router, w_gate=w_gate, w_up=w_up, w_down=w_down, routes=routes)


def attention_rows(query_rows, new_pair, cache_rows, live_count):
    row_total = query_rows.shape[0]
    query_heads = query_rows.reshape(row_total, QPK, HD).astype(jnp.float32)
    keys_cached = cache_rows[:, :, :HD].astype(jnp.float32)
    values_cached = cache_rows[:, :, HD:].astype(jnp.float32)
    key_fresh = new_pair[:, :HD].astype(jnp.float32)
    value_fresh = new_pair[:, HD:].astype(jnp.float32)
    factor = 1.0 / math.sqrt(HD)
    scores = jnp.einsum('rqd,rpd->rqp', query_heads, keys_cached) * factor
    own_score = jnp.einsum('rqd,rd->rq', query_heads, key_fresh) * factor
    live = jnp.arange(WIN)[None, None, :] < live_count[:, None, None]
    masked = jnp.where(live, scores, -jnp.inf)
    top_score = jnp.maximum(lax.optimization_barrier(jnp.max(masked, axis=2)), own_score)
    weight_cached = jnp.exp(masked - top_score[:, :, None])
    weight_own = jnp.exp(own_score - top_score)
    total = lax.optimization_barrier(jnp.sum(weight_cached, axis=2)) + weight_own
    prob_cached = lax.optimization_barrier((weight_cached / total[:, :, None]).astype(jnp.bfloat16))
    prob_own = lax.optimization_barrier((weight_own / total).astype(jnp.bfloat16))
    mixed = jnp.einsum('rqp,rpd->rqd', prob_cached.astype(jnp.float32), values_cached)
    mixed = mixed + prob_own.astype(jnp.float32)[:, :, None] * value_fresh[:, None, :]
    return mixed.astype(jnp.bfloat16).reshape(row_total, QPK * HD)

def expert_block(operands):
    rows_in, gate_full, up_full, down_full = operands
    gate_hidden = jnp.dot(rows_in, gate_full, preferred_element_type=jnp.float32)
    up_hidden = jnp.dot(rows_in, up_full, preferred_element_type=jnp.float32)
    active = ((up_hidden + 1.0) * gate_hidden * jax.nn.sigmoid(1.702 * gate_hidden)).astype(jnp.bfloat16)
    return jnp.dot(active, down_full, preferred_element_type=jnp.float32)

def reference(queries, new_kv, cache, lengths, residual, o_proj, router, w_gate, w_up, w_down, routes):
    request_count = residual.shape[1]
    block_count = request_count // REQ_DEV
    gate_full = w_gate.reshape(EXPERTS, SPLIT, D, FFS).transpose(0, 2, 1, 3).reshape(EXPERTS, D, SPLIT * FFS)
    up_full = w_up.reshape(EXPERTS, SPLIT, D, FFS).transpose(0, 2, 1, 3).reshape(EXPERTS, D, SPLIT * FFS)
    down_full = w_down.reshape(EXPERTS, SPLIT * FFS, D)
    attended_list = []
    layer_list = []
    for batch_index in range(MB):
        live_rows = jnp.tile(lengths[batch_index], KVH)
        mixed = attention_rows(queries[batch_index], new_kv[batch_index], cache[batch_index], live_rows)
        heads_all = mixed.reshape(KVH, request_count, QPK * HD).transpose(1, 0, 2).reshape(request_count, KVH * QPK * HD)
        attended = (residual[batch_index].astype(jnp.float32) + jnp.dot(heads_all, o_proj, preferred_element_type=jnp.float32)).astype(jnp.bfloat16)
        attended_wide = attended.astype(jnp.float32)
        normed = (attended_wide * lax.rsqrt(lax.optimization_barrier(jnp.mean(attended_wide * attended_wide, axis=1, keepdims=True)) + 1e-05)).astype(jnp.bfloat16)
        logits = jnp.dot(normed, router, preferred_element_type=jnp.float32)
        route_ids = routes[batch_index]
        chosen = jnp.take_along_axis(logits, route_ids, axis=1)
        gates = 1.0 / lax.optimization_barrier(jnp.sum(jnp.exp(chosen[:, None, :] - chosen[:, :, None]), axis=2))
        one_hot = (route_ids[:, :, None] == jnp.arange(EXPERTS, dtype=jnp.int32)[None, None, :]).astype(jnp.int32)
        by_block = one_hot.reshape(block_count, REQ_DEV * TOPK, EXPERTS)
        earlier = jnp.cumsum(by_block, axis=1) - by_block
        ranks = lax.optimization_barrier(jnp.sum(earlier * by_block, axis=2)).reshape(request_count, TOPK)
        block_of_row = (jnp.arange(request_count, dtype=jnp.int32) // REQ_DEV)[:, None]
        slot_index = (route_ids * (block_count * CAP) + block_of_row * CAP + ranks).astype(jnp.int32)
        buffer = jnp.zeros((EXPERTS * block_count * CAP, D), jnp.bfloat16)
        buffer = buffer.at[slot_index.reshape(-1)].set(jnp.repeat(normed, TOPK, axis=0))
        expert_rows = buffer.reshape(EXPERTS, block_count * CAP, D)
        produced = lax.map(expert_block, (expert_rows, gate_full, up_full, down_full))
        flat_out = produced.reshape(EXPERTS * block_count * CAP, D)
        picked = jnp.take(flat_out, slot_index, axis=0)
        mixture = lax.optimization_barrier(jnp.sum(gates[:, :, None] * picked, axis=1))
        layer = (attended_wide + mixture).astype(jnp.bfloat16)
        attended_list.append(attended)
        layer_list.append(layer)
    return (jnp.stack(attended_list), jnp.stack(layer_list))
```

```python
import functools
import math

import jax
import jax.numpy as jnp
from jax import lax
from jax.experimental import pallas as pl
from jax.experimental.pallas import tpu as pltpu
from jax.sharding import PartitionSpec as P

HD = 64
LANES = 128
EPS = 1e-05
MESH = pl.DeviceIdType.MESH


def flip(value, mask):
    bit = 1
    result = value
    while bit <= mask:
        if mask & bit:
            result = result + bit - 2 * bit * ((value // bit) % 2)
        bit *= 2
    return result


def exclusive(left, right, bits):
    result = left * 0
    for b in range(bits):
        x = (left // (1 << b)) % 2
        y = (right // (1 << b)) % 2
        result = result + (x + y - 2 * x * y) * (1 << b)
    return result


def layer_kernel(
    cfg,
    q_ref, nk_ref, bias_ref, cache_ref, res_ref, o_ref, router_ref, gate_ref, up_ref, down_ref, routes_ref,
    att_ref, lay_ref,
    cache_v, o_v, gate_v, up_v, down_v, mixed_v, heads_v, block_v, lhs_v,
    acc0, acc1, send0, send1, first0, first1, second0, second1, rows0, rows1, gates_v, wide_v, out0, out1,
    cache_sem, load_sem, swap_sem, rs_sem, ag_sem,
):
    n, levels, group, width, subs, splits, per_expert = cfg
    me = lax.axis_index("req")
    mine = me % group
    accs, sends = (acc0, acc1), (send0, send1)
    landings = ((first0, first1), (second0, second1))
    rows = (rows0, rows1)
    outs = (out0, out1)
    orders = [list(range(levels)), list(range(levels))]
    if levels > 2:
        orders[1][1], orders[1][2] = 2, 1
    starts = (0, splits[0])
    batches = cache_ref.shape[0]
    rank = levels

    def cache_copy(s, m):
        return pltpu.make_async_copy(
            cache_ref.at[m, pl.ds(s * 8, 8)], cache_v.at[s, m], cache_sem.at[s, m]
        )

    for s in range(subs):
        for m in range(batches):
            cache_copy(s, m).start()
    loads = [
        pltpu.make_async_copy(src, dst, load_sem.at[i])
        for i, (src, dst) in enumerate(
            ((o_ref, o_v), (gate_ref, gate_v), (up_ref, up_v), (down_ref, down_v))
        )
    ]
    for load in loads:
        load.start()

    masks = sorted({1 << d for d in range(levels)} | set(range(1, group)))
    barrier = pltpu.get_barrier_semaphore()
    for mask in masks:
        pl.semaphore_signal(barrier, inc=1, device_id={"req": flip(me, mask)}, device_id_type=MESH)

    factor = 1.0 / math.sqrt(HD)
    lane = lax.broadcasted_iota(jnp.int32, (16, LANES), 1)

    def attend(s, carry):
        for m in range(batches):
            cache_copy(s, m).wait()
        scores = []
        for r in range(16):
            keys = cache_v[s, r // 8, r % 8]
            scores.append(
                lax.dot_general(
                    q_ref[s * 16 + r], keys, (((1,), (1,)), ((), ())), preferred_element_type=jnp.float32
                )
            )
        scores = jnp.concatenate(scores, axis=0) * factor
        bias = jnp.broadcast_to(bias_ref[s][:, None, :], (16, 8, LANES)).reshape(128, LANES)
        fresh = jnp.broadcast_to(nk_ref[s].astype(jnp.float32)[:, None, :], (16, 8, LANES)).reshape(128, LANES)
        query = q_ref[pl.ds(s * 16, 16)].astype(jnp.float32).reshape(128, LANES)
        own = jnp.sum(query * fresh, axis=1, keepdims=True) * factor
        masked = scores + bias
        top = jnp.maximum(jnp.max(masked, axis=1, keepdims=True), own)
        weight = jnp.exp(masked - top)
        weight_own = jnp.exp(own - top)
        total = jnp.sum(weight, axis=1, keepdims=True) + weight_own
        probs = weight / total
        prob_own = (weight_own / total).astype(jnp.bfloat16).astype(jnp.float32)
        mixed = []
        for r in range(16):
            mixed.append(
                jnp.dot(
                    probs[r * 8 : r * 8 + 8].astype(jnp.bfloat16),
                    cache_v[s, r // 8, r % 8],
                    preferred_element_type=jnp.float32,
                )
            )
        mixed_v[...] = jnp.concatenate(mixed, axis=0) + prob_own * fresh
        head = [mixed_v[pl.ds(h, 16, stride=8), :] for h in range(8)]
        if width >= LANES:
            for j in range(4):
                pair = jnp.where(lane < HD, pltpu.roll(head[2 * j], HD, 1), head[2 * j + 1])
                dest, col = j * LANES // width, j * LANES % width
                heads_v[dest, s, :, col : col + LANES] = pair.astype(jnp.bfloat16)
        else:
            for h in range(8):
                heads_v[h, s] = pltpu.roll(head[h], HD, 1)[:, :HD].astype(jnp.bfloat16)
        return carry

    lax.fori_loop(0, subs, attend, 0)
    pl.semaphore_wait(barrier, len(masks))

    swaps = []
    for j in range(1, group):
        partner = flip(me, j)
        swap = pltpu.make_async_remote_copy(
            src_ref=heads_v.at[partner % group],
            dst_ref=block_v.at[j],
            send_sem=swap_sem.at[0, j],
            recv_sem=swap_sem.at[1, j],
            device_id={"req": partner},
            device_id_type=MESH,
        )
        swap.start()
        swaps.append(swap)
    block_v[0] = heads_v[mine]
    loads[0].wait()
    for swap in swaps:
        swap.wait()
    group_bits = group.bit_length() - 1
    for place in range(n):
        mask = sum(((place >> (levels - 1 - d)) & 1) << d for d in range(levels))
        dest = flip(me, mask)
        slot = exclusive(dest // subs % group, mine, group_bits)
        lhs_v[place] = block_v[slot, dest % subs]

    def region(order, level, bit):
        index = [slice(None)] * rank
        for d in order[:level]:
            index[d] = 0
        index[order[level]] = bit
        return tuple(index)

    def scatter_sum(phase):
        landing = landings[phase]
        copies = {}
        for level in range(levels):
            for c in range(2):
                order = orders[c]
                if level:
                    copies[level - 1, c].wait_recv()
                    done = region(order, level - 1, 1)
                    kept = region(order, level - 1, 0)
                    accs[c][kept] = accs[c][kept] + landing[c][done].astype(jnp.float32)
                out = region(order, level, 1)
                sends[c][out] = accs[c][out].astype(jnp.bfloat16)
                copies[level, c] = pltpu.make_async_remote_copy(
                    src_ref=sends[c].at[out],
                    dst_ref=landing[c].at[out],
                    send_sem=rs_sem.at[phase, 0, level, c],
                    recv_sem=rs_sem.at[phase, 1, level, c],
                    device_id={"req": flip(me, 1 << order[level])},
                    device_id_type=MESH,
                )
                copies[level, c].start()
        total = []
        for c in range(2):
            copies[levels - 1, c].wait_recv()
            last = region(orders[c], levels - 1, 1)
            kept = region(orders[c], levels - 1, 0)
            total.append(accs[c][kept] + landing[c][last].astype(jnp.float32))
        for copy in copies.values():
            copy.wait_send()
        return total

    lhs = lhs_v[...].reshape(n * 16, width)
    for c in range(2):
        part = jnp.dot(lhs, o_v[:, starts[c] : starts[c] + splits[c]], preferred_element_type=jnp.float32)
        accs[c][...] = part.reshape(accs[c].shape)
    summed = scatter_sum(0)

    own_place = (0,) * rank
    depth = splits[0] + splits[1]
    square = jnp.zeros((16, 1), jnp.float32)
    attended = []
    for c in range(2):
        cols = slice(starts[c], starts[c] + splits[c])
        held = jnp.concatenate([res_ref[m, :, cols].astype(jnp.float32) for m in range(2)], axis=0)
        value = (held + summed[c]).astype(jnp.bfloat16)
        for m in range(2):
            att_ref[m, :, cols] = value[m * 8 : m * 8 + 8]
        value = value.astype(jnp.float32)
        wide_v[:, cols] = value
        attended.append(value)
        square = square + jnp.sum(value * value, axis=1, keepdims=True)
    scale = lax.rsqrt(square / depth + EPS)
    logits = 0.0
    for c in range(2):
        normed = (attended[c] * scale).astype(jnp.bfloat16)
        rows[c][own_place] = normed
        logits = logits + jnp.dot(
            normed, router_ref[starts[c] : starts[c] + splits[c], :], preferred_element_type=jnp.float32
        )
    experts = router_ref.shape[1]
    ids = lax.broadcasted_iota(jnp.int32, (16, experts), 1)
    routes = routes_ref[...]
    named = jnp.zeros((16, experts), jnp.float32)
    for t in range(routes_ref.shape[1]):
        named = jnp.where(ids == routes[:, t : t + 1], 1.0, named)
    live = jnp.where(named > 0.0, logits, -jnp.inf)
    power = jnp.exp(live - jnp.max(live, axis=1, keepdims=True))
    gates = power / jnp.sum(power, axis=1, keepdims=True)
    gates_v[own_place] = jnp.concatenate([gates, jnp.zeros((16, LANES - experts), jnp.float32)], axis=1)

    streams = ((rows0, orders[0]), (rows1, orders[1]), (gates_v, orders[0]))
    copies = {}
    for level in reversed(range(levels)):
        for c, (ref, order) in enumerate(streams):
            if level < levels - 1:
                copies[level + 1, c].wait_recv()
            copies[level, c] = pltpu.make_async_remote_copy(
                src_ref=ref.at[region(order, level, 0)],
                dst_ref=ref.at[region(order, level, 1)],
                send_sem=ag_sem.at[0, level, c],
                recv_sem=ag_sem.at[1, level, c],
                device_id={"req": flip(me, 1 << order[level])},
                device_id_type=MESH,
            )
            copies[level, c].start()
    for c in range(3):
        copies[0, c].wait_recv()
    for copy in copies.values():
        copy.wait_send()
    for load in loads[1:]:
        load.wait()

    entries = gate_ref.shape[0]
    expert = me * entries // per_expert
    tiles = n // 16
    tile_bits = tiles.bit_length() - 1

    def tile_body(tile, carry):
        lead = tuple((tile // (1 << (tile_bits - 1 - b))) % 2 for b in range(tile_bits))
        at = lead + (slice(None),) * (rank - tile_bits)

        def entry_body(j, inner):
            hidden = []
            for weights in (gate_v, up_v):
                value = 0.0
                for c in range(2):
                    x = rows[c][at].reshape(256, splits[c])
                    value = value + jnp.dot(
                        x, weights[j, starts[c] : starts[c] + splits[c], :], preferred_element_type=jnp.float32
                    )
                hidden.append(value)
            g, u = hidden
            active = ((u + 1.0) * g * jax.nn.sigmoid(1.702 * g)).astype(jnp.bfloat16)
            for c in range(2):
                part = jnp.dot(
                    active, down_v[j, :, starts[c] : starts[c] + splits[c]], preferred_element_type=jnp.float32
                )
                outs[c][...] = jnp.where(j == 0, 0.0, outs[c][...]) + part
            return inner

        lax.fori_loop(0, entries, entry_body, 0)
        wide_gates = gates_v[at].reshape(256, LANES)
        column = lax.broadcasted_iota(jnp.int32, (256, LANES), 1)
        gate = jnp.sum(jnp.where(column == expert, wide_gates, 0.0), axis=1, keepdims=True)
        for c in range(2):
            part = jnp.where(gate > 0.0, outs[c][...] * gate, 0.0)
            accs[c][at] = part.reshape((2,) * (rank - tile_bits) + (16, splits[c]))
        return carry

    for c in range(2):
        outs[c][...] = jnp.zeros_like(outs[c])
    lax.fori_loop(0, tiles, tile_body, 0)
    mixture = scatter_sum(1)
    for c in range(2):
        cols = slice(starts[c], starts[c] + splits[c])
        value = (wide_v[:, cols] + mixture[c]).astype(jnp.bfloat16)
        for m in range(2):
            lay_ref[m, :, cols] = value[m * 8 : m * 8 + 8]


def shards(queries, new_kv, cache, lengths, residual, o_proj, router, w_gate, w_up, w_down, routes):
    n = lax.axis_size("req")
    me = lax.axis_index("req")
    levels = n.bit_length() - 1
    batches, local, q_cols = queries.shape
    depth = residual.shape[2]
    own_rows = residual.shape[1]
    window = cache.shape[2]
    width = o_proj.shape[0]
    group = q_cols // width
    subs = local // own_rows
    heads = q_cols // HD
    per_expert = max(1, n * w_gate.shape[0] // router.shape[1])
    cut = (depth // 2 + LANES - 1) // LANES * LANES
    splits = (cut, depth - cut)

    def by_place(x):
        x = x.reshape((batches, subs, own_rows) + x.shape[2:])
        x = jnp.swapaxes(x, 0, 1)
        return x.reshape((subs, batches * own_rows) + x.shape[3:])

    live = lax.dynamic_slice_in_dim(lengths, me % group * local, local, 1)
    bias = jnp.where(jnp.arange(window)[None, None, :] < live[:, :, None], 0.0, -jnp.inf).astype(jnp.float32)
    query = jnp.pad(queries.reshape(batches, local, heads, HD), ((0, 0), (0, 0), (0, 0), (0, HD)))
    query = by_place(query).reshape(batches * local, heads, 2 * HD)

    cube = (2,) * levels
    f32, b16 = jnp.float32, jnp.bfloat16
    rows = batches * own_rows
    vmem = pl.BlockSpec(memory_space=pltpu.VMEM)
    hbm = pl.BlockSpec(memory_space=pl.ANY)

    def pair(dtype):
        return [pltpu.VMEM(cube + (rows, s), dtype) for s in splits]

    scratch = [
        pltpu.VMEM((subs, batches, own_rows) + cache.shape[2:], b16),
        pltpu.VMEM(o_proj.shape, b16),
        pltpu.VMEM(w_gate.shape, b16),
        pltpu.VMEM(w_up.shape, b16),
        pltpu.VMEM(w_down.shape, b16),
        pltpu.VMEM((rows * heads, LANES), f32),
        pltpu.VMEM((group, subs, rows, width), b16),
        pltpu.VMEM((group, subs, rows, width), b16),
        pltpu.VMEM((n, rows, width), b16),
        *pair(f32), *pair(b16), *pair(b16), *pair(b16), *pair(b16),
        pltpu.VMEM(cube + (rows, LANES), f32),
        pltpu.VMEM((rows, depth), f32),
        *[pltpu.VMEM((256, s), f32) for s in splits],
        pltpu.SemaphoreType.DMA((subs, batches)),
        pltpu.SemaphoreType.DMA((4,)),
        pltpu.SemaphoreType.DMA((2, group)),
        pltpu.SemaphoreType.DMA((2, 2, levels, 2)),
        pltpu.SemaphoreType.DMA((2, levels, 3)),
    ]
    out = jax.ShapeDtypeStruct(residual.shape, b16)
    return pl.pallas_call(
        functools.partial(layer_kernel, (n, levels, group, width, subs, splits, per_expert)),
        out_shape=(out, out),
        in_specs=[vmem, vmem, vmem, hbm, vmem, hbm, vmem, hbm, hbm, hbm, vmem],
        out_specs=(vmem, vmem),
        scratch_shapes=scratch,
        compiler_params=pltpu.CompilerParams(
            collective_id=0, has_side_effects=True, vmem_limit_bytes=67043328
        ),
        name="moe_layer",
    )(
        query, by_place(new_kv), by_place(bias), cache, residual, o_proj, router, w_gate, w_up, w_down,
        routes.reshape(rows, routes.shape[2]),
    )


def solution(mesh):
    placed = (
        P(None, ("groups", "req"), None),
        P(None, ("groups", "req"), None),
        P(None, ("groups", "req"), None, None),
        P(None, "groups"),
        P(None, ("groups", "req"), None),
        P("req", None),
        P(),
        P("req", None, None),
        P("req", None, None),
        P("req", None, None),
        P(None, ("groups", "req"), None),
    )
    if tuple(mesh.axis_names) != ("groups", "req"):
        raise ValueError("mesh axes")
    return jax.shard_map(
        shards,
        mesh=mesh,
        in_specs=placed,
        out_specs=(P(None, ("groups", "req"), None), P(None, ("groups", "req"), None)),
        check_vma=False,
    )
```

```python
import functools
import math

import jax
import jax.numpy as jnp
from jax import lax
from jax.experimental import pallas as pl
from jax.experimental.pallas import tpu as pltpu
from jax.sharding import PartitionSpec as P

HD = 64
LANES = 128
EPS = 1e-05
MESH = pl.DeviceIdType.MESH


def flip(value, mask):
    bit = 1
    result = value
    while bit <= mask:
        if mask & bit:
            result = result + bit - 2 * bit * ((value // bit) % 2)
        bit *= 2
    return result


def exclusive(left, right, bits):
    result = left * 0
    for b in range(bits):
        x = (left // (1 << b)) % 2
        y = (right // (1 << b)) % 2
        result = result + (x + y - 2 * x * y) * (1 << b)
    return result


def dot_t(left, right):
    return lax.dot_general(left, right, (((1,), (1,)), ((), ())), preferred_element_type=jnp.float32)


def layer_kernel(
    cfg,
    q_ref, nk_ref, len_ref, cache_ref, res_ref, o_ref, router_ref, gate_ref, up_ref, down_ref, routes_ref,
    att_ref, lay_ref,
    cache_v, o_v, gate_v, up_v, down_v, query_v, mixed_v, heads_v, block_v, lhs_v,
    acc0, acc1, send0, send1, first0, first1, second0, second1, rows0, rows1, gates_v, wide_v, out0, out1,
    cache_sem, load_sem, swap_sem, rs_sem, ag_sem,
):
    n, levels, group, width, subs, splits, per_expert = cfg
    me = lax.axis_index("req")
    mine = me % group
    accs, sends = (acc0, acc1), (send0, send1)
    landings = ((first0, first1), (second0, second1))
    rows = (rows0, rows1)
    outs = (out0, out1)
    orders = [list(range(levels)), list(range(levels))]
    if levels > 2:
        orders[1][1], orders[1][2] = 2, 1
    starts = (0, splits[0])
    batches = cache_ref.shape[0]
    rank = levels

    def cache_copy(s, m):
        return pltpu.make_async_copy(
            cache_ref.at[m, pl.ds(s * 8, 8)], cache_v.at[s, m], cache_sem.at[s, m]
        )

    for s in range(subs):
        for m in range(batches):
            cache_copy(s, m).start()
    loads = [
        pltpu.make_async_copy(src, dst, load_sem.at[i])
        for i, (src, dst) in enumerate(
            ((o_ref, o_v), (gate_ref, gate_v), (up_ref, up_v), (down_ref, down_v))
        )
    ]
    for load in loads:
        load.start()

    masks = sorted({1 << d for d in range(levels)} | set(range(1, group)))
    barrier = pltpu.get_barrier_semaphore()
    for mask in masks:
        pl.semaphore_signal(barrier, inc=1, device_id={"req": flip(me, mask)}, device_id_type=MESH)

    factor = 1.0 / math.sqrt(HD)
    lane = lax.broadcasted_iota(jnp.int32, (16, LANES), 1)
    position = lax.broadcasted_iota(jnp.int32, (8, LANES), 1)
    first = mine * subs * 8

    def attend(s, carry):
        for m in range(batches):
            cache_copy(s, m).wait()
        here = pl.ds(pl.multiple_of(s * 8, 8), 8)
        fresh = jnp.concatenate([nk_ref[m, here, :].astype(jnp.float32) for m in range(batches)], axis=0)
        fresh = jnp.broadcast_to(fresh[:, None, :], (16, 8, LANES)).reshape(128, LANES)
        for j in range(4):
            pair = jnp.concatenate(
                [q_ref[m, here, j * LANES : (j + 1) * LANES].astype(jnp.float32) for m in range(batches)], axis=0
            )
            query_v[pl.ds(2 * j, 16, stride=8), :] = jnp.where(lane < HD, pair, 0.0)
            query_v[pl.ds(2 * j + 1, 16, stride=8), :] = jnp.where(lane < HD, pltpu.roll(pair, HD, 1), 0.0)
        masked = []
        for r in range(16):
            score = dot_t(query_v[r * 8 : r * 8 + 8, :].astype(jnp.bfloat16), cache_v[s, r // 8, r % 8])
            live = position < len_ref[r // 8, first + s * 8 + r % 8]
            masked.append(jnp.where(live, score * factor, -jnp.inf))
        masked = jnp.concatenate(masked, axis=0)
        own = jnp.sum(query_v[...] * fresh, axis=1, keepdims=True) * factor
        top = jnp.maximum(jnp.max(masked, axis=1, keepdims=True), own)
        weight = jnp.exp(masked - top)
        weight_own = jnp.exp(own - top)
        total = jnp.sum(weight, axis=1, keepdims=True) + weight_own
        probs = weight / total
        prob_own = (weight_own / total).astype(jnp.bfloat16).astype(jnp.float32)
        mixed = []
        for r in range(16):
            mixed.append(
                jnp.dot(
                    probs[r * 8 : r * 8 + 8].astype(jnp.bfloat16),
                    cache_v[s, r // 8, r % 8],
                    preferred_element_type=jnp.float32,
                )
            )
        mixed_v[...] = jnp.concatenate(mixed, axis=0) + prob_own * fresh
        head = [mixed_v[pl.ds(h, 16, stride=8), :] for h in range(8)]
        if width >= LANES:
            for j in range(4):
                pair = jnp.where(lane < HD, pltpu.roll(head[2 * j], HD, 1), head[2 * j + 1])
                dest, col = j * LANES // width, j * LANES % width
                heads_v[dest, s, :, col : col + LANES] = pair.astype(jnp.bfloat16)
        else:
            for h in range(8):
                heads_v[h, s] = pltpu.roll(head[h], HD, 1)[:, :HD].astype(jnp.bfloat16)
        return carry

    lax.fori_loop(0, subs, attend, 0)
    pl.semaphore_wait(barrier, len(masks))

    swaps = []
    for j in range(1, group):
        partner = flip(me, j)
        swap = pltpu.make_async_remote_copy(
            src_ref=heads_v.at[partner % group],
            dst_ref=block_v.at[j],
            send_sem=swap_sem.at[0, j],
            recv_sem=swap_sem.at[1, j],
            device_id={"req": partner},
            device_id_type=MESH,
        )
        swap.start()
        swaps.append(swap)
    block_v[0] = heads_v[mine]
    loads[0].wait()
    for swap in swaps:
        swap.wait()
    group_bits = group.bit_length() - 1
    for place in range(n):
        mask = sum(((place >> (levels - 1 - d)) & 1) << d for d in range(levels))
        dest = flip(me, mask)
        slot = exclusive(dest // subs % group, mine, group_bits)
        lhs_v[place] = block_v[slot, dest % subs]

    def region(order, level, bit):
        index = [slice(None)] * rank
        for d in order[:level]:
            index[d] = 0
        index[order[level]] = bit
        return tuple(index)

    def scatter_sum(phase):
        landing = landings[phase]
        copies = {}
        for level in range(levels):
            for c in range(2):
                order = orders[c]
                if level:
                    copies[level - 1, c].wait_recv()
                    done = region(order, level - 1, 1)
                    kept = region(order, level - 1, 0)
                    accs[c][kept] = accs[c][kept] + landing[c][done].astype(jnp.float32)
                out = region(order, level, 1)
                sends[c][out] = accs[c][out].astype(jnp.bfloat16)
                copies[level, c] = pltpu.make_async_remote_copy(
                    src_ref=sends[c].at[out],
                    dst_ref=landing[c].at[out],
                    send_sem=rs_sem.at[phase, 0, level, c],
                    recv_sem=rs_sem.at[phase, 1, level, c],
                    device_id={"req": flip(me, 1 << order[level])},
                    device_id_type=MESH,
                )
                copies[level, c].start()
        total = []
        for c in range(2):
            copies[levels - 1, c].wait_recv()
            last = region(orders[c], levels - 1, 1)
            kept = region(orders[c], levels - 1, 0)
            total.append(accs[c][kept] + landing[c][last].astype(jnp.float32))
        for copy in copies.values():
            copy.wait_send()
        return total

    lhs = lhs_v[...].reshape(n * 16, width)
    for c in range(2):
        part = dot_t(lhs, o_v[starts[c] : starts[c] + splits[c], :])
        accs[c][...] = part.reshape(accs[c].shape)
    summed = scatter_sum(0)

    own_place = (0,) * rank
    depth = splits[0] + splits[1]
    square = jnp.zeros((16, 1), jnp.float32)
    attended = []
    for c in range(2):
        cols = slice(starts[c], starts[c] + splits[c])
        held = jnp.concatenate([res_ref[m, :, cols].astype(jnp.float32) for m in range(2)], axis=0)
        value = (held + summed[c]).astype(jnp.bfloat16)
        for m in range(2):
            att_ref[m, :, cols] = value[m * 8 : m * 8 + 8]
        value = value.astype(jnp.float32)
        wide_v[:, cols] = value
        attended.append(value)
        square = square + jnp.sum(value * value, axis=1, keepdims=True)
    scale = lax.rsqrt(square / depth + EPS)
    logits = 0.0
    for c in range(2):
        normed = (attended[c] * scale).astype(jnp.bfloat16)
        rows[c][own_place] = normed
        logits = logits + dot_t(normed, router_ref[:, starts[c] : starts[c] + splits[c]])
    experts = router_ref.shape[0]
    ids = lax.broadcasted_iota(jnp.int32, (16, experts), 1).astype(jnp.float32)
    row = lax.broadcasted_iota(jnp.int32, (16, 8), 0)
    col = lax.broadcasted_iota(jnp.int32, (16, 8), 1)
    routes = 0.0
    for m in range(batches):
        pick = jnp.where(row == col + m * 8, 1.0, 0.0).astype(jnp.bfloat16)
        routes = routes + dot_t(pick, routes_ref[m].astype(jnp.float32).astype(jnp.bfloat16))
    named = jnp.zeros((16, experts), jnp.float32)
    for t in range(routes_ref.shape[1]):
        named = jnp.where(ids == routes[:, t : t + 1], 1.0, named)
    live = jnp.where(named > 0.0, logits, -jnp.inf)
    power = jnp.exp(live - jnp.max(live, axis=1, keepdims=True))
    gates = power / jnp.sum(power, axis=1, keepdims=True)
    gates_v[own_place] = jnp.concatenate([gates, jnp.zeros((16, LANES - experts), jnp.float32)], axis=1)

    streams = ((rows0, orders[0]), (rows1, orders[1]), (gates_v, orders[0]))
    copies = {}
    for level in reversed(range(levels)):
        for c, (ref, order) in enumerate(streams):
            if level < levels - 1:
                copies[level + 1, c].wait_recv()
            copies[level, c] = pltpu.make_async_remote_copy(
                src_ref=ref.at[region(order, level, 0)],
                dst_ref=ref.at[region(order, level, 1)],
                send_sem=ag_sem.at[0, level, c],
                recv_sem=ag_sem.at[1, level, c],
                device_id={"req": flip(me, 1 << order[level])},
                device_id_type=MESH,
            )
            copies[level, c].start()
    for c in range(3):
        copies[0, c].wait_recv()
    for copy in copies.values():
        copy.wait_send()
    for load in loads[1:]:
        load.wait()

    entries = gate_ref.shape[0]
    expert = me * entries // per_expert
    tiles = n // 16
    tile_bits = tiles.bit_length() - 1

    def tile_body(tile, carry):
        lead = tuple((tile // (1 << (tile_bits - 1 - b))) % 2 for b in range(tile_bits))
        at = lead + (slice(None),) * (rank - tile_bits)

        def entry_body(j, inner):
            hidden = []
            for weights in (gate_v, up_v):
                value = 0.0
                for c in range(2):
                    x = rows[c][at].reshape(256, splits[c])
                    value = value + dot_t(x, weights[j, :, starts[c] : starts[c] + splits[c]])
                hidden.append(value)
            g, u = hidden
            active = ((u + 1.0) * g * jax.nn.sigmoid(1.702 * g)).astype(jnp.bfloat16)
            for c in range(2):
                part = jnp.dot(
                    active, down_v[j, :, starts[c] : starts[c] + splits[c]], preferred_element_type=jnp.float32
                )
                outs[c][...] = jnp.where(j == 0, 0.0, outs[c][...]) + part
            return inner

        lax.fori_loop(0, entries, entry_body, 0)
        wide_gates = gates_v[at].reshape(256, LANES)
        column = lax.broadcasted_iota(jnp.int32, (256, LANES), 1)
        gate = jnp.sum(jnp.where(column == expert, wide_gates, 0.0), axis=1, keepdims=True)
        for c in range(2):
            part = jnp.where(gate > 0.0, outs[c][...] * gate, 0.0)
            accs[c][at] = part.reshape((2,) * (rank - tile_bits) + (16, splits[c]))
        return carry

    for c in range(2):
        outs[c][...] = jnp.zeros_like(outs[c])
    lax.fori_loop(0, tiles, tile_body, 0)
    mixture = scatter_sum(1)
    for c in range(2):
        cols = slice(starts[c], starts[c] + splits[c])
        value = (wide_v[:, cols] + mixture[c]).astype(jnp.bfloat16)
        for m in range(2):
            lay_ref[m, :, cols] = value[m * 8 : m * 8 + 8]


def shards(queries, new_kv, cache, lengths, residual, o_proj, router, w_gate, w_up, w_down, routes):
    n = lax.axis_size("req")
    levels = n.bit_length() - 1
    batches, local, q_cols = queries.shape
    depth = residual.shape[2]
    own_rows = residual.shape[1]
    width = o_proj.shape[0]
    group = q_cols // width
    subs = local // own_rows
    heads = q_cols // HD
    per_expert = max(1, n * w_gate.shape[0] // router.shape[1])
    cut = (depth // 2 + LANES - 1) // LANES * LANES
    splits = (cut, depth - cut)

    gate_t, up_t = jnp.swapaxes(w_gate, 1, 2), jnp.swapaxes(w_up, 1, 2)
    cube = (2,) * levels
    f32, b16 = jnp.float32, jnp.bfloat16
    rows = batches * own_rows
    vmem = pl.BlockSpec(memory_space=pltpu.VMEM)
    smem = pl.BlockSpec(memory_space=pltpu.SMEM)
    hbm = pl.BlockSpec(memory_space=pl.ANY)

    def pair(dtype):
        return [pltpu.VMEM(cube + (rows, s), dtype) for s in splits]

    scratch = [
        pltpu.VMEM((subs, batches, own_rows) + cache.shape[2:], b16),
        pltpu.VMEM(o_proj.shape[::-1], b16),
        pltpu.VMEM(gate_t.shape, b16),
        pltpu.VMEM(up_t.shape, b16),
        pltpu.VMEM(w_down.shape, b16),
        pltpu.VMEM((rows * heads, LANES), f32),
        pltpu.VMEM((rows * heads, LANES), f32),
        pltpu.VMEM((group, subs, rows, width), b16),
        pltpu.VMEM((group, subs, rows, width), b16),
        pltpu.VMEM((n, rows, width), b16),
        *pair(f32), *pair(b16), *pair(b16), *pair(b16), *pair(b16),
        pltpu.VMEM(cube + (rows, LANES), f32),
        pltpu.VMEM((rows, depth), f32),
        *[pltpu.VMEM((256, s), f32) for s in splits],
        pltpu.SemaphoreType.DMA((subs, batches)),
        pltpu.SemaphoreType.DMA((4,)),
        pltpu.SemaphoreType.DMA((2, group)),
        pltpu.SemaphoreType.DMA((2, 2, levels, 2)),
        pltpu.SemaphoreType.DMA((2, levels, 3)),
    ]
    out = jax.ShapeDtypeStruct(residual.shape, b16)
    return pl.pallas_call(
        functools.partial(layer_kernel, (n, levels, group, width, subs, splits, per_expert)),
        out_shape=(out, out),
        in_specs=[vmem, vmem, smem, hbm, vmem, hbm, vmem, hbm, hbm, hbm, vmem],
        out_specs=(vmem, vmem),
        scratch_shapes=scratch,
        compiler_params=pltpu.CompilerParams(
            collective_id=0, has_side_effects=True, vmem_limit_bytes=67043328
        ),
        name="moe_layer",
    )(
        queries, new_kv, lengths, cache, residual, o_proj.T, router.T, gate_t, up_t, w_down,
        jnp.swapaxes(routes, 1, 2),
    )


def solution(mesh):
    placed = (
        P(None, ("groups", "req"), None),
        P(None, ("groups", "req"), None),
        P(None, ("groups", "req"), None, None),
        P(None, "groups"),
        P(None, ("groups", "req"), None),
        P("req", None),
        P(),
        P("req", None, None),
        P("req", None, None),
        P("req", None, None),
        P(None, ("groups", "req"), None),
    )
    if tuple(mesh.axis_names) != ("groups", "req"):
        raise ValueError("mesh axes")
    return jax.shard_map(
        shards,
        mesh=mesh,
        in_specs=placed,
        out_specs=(P(None, ("groups", "req"), None), P(None, ("groups", "req"), None)),
        check_vma=False,
    )
```

```python
import functools
import math

import jax
import jax.numpy as jnp
from jax import lax
from jax.experimental import pallas as pl
from jax.experimental.pallas import tpu as pltpu
from jax.sharding import PartitionSpec as P

HD = 64
LANES = 128
EPS = 1e-05
MESH = pl.DeviceIdType.MESH


def flip(value, mask):
    bit = 1
    result = value
    while bit <= mask:
        if mask & bit:
            result = result + bit - 2 * bit * ((value // bit) % 2)
        bit *= 2
    return result


def exclusive(left, right, bits):
    result = left * 0
    for b in range(bits):
        x = (left // (1 << b)) % 2
        y = (right // (1 << b)) % 2
        result = result + (x + y - 2 * x * y) * (1 << b)
    return result


def dot_t(left, right):
    return lax.dot_general(left, right, (((1,), (1,)), ((), ())), preferred_element_type=jnp.float32)


def layer_kernel(
    cfg,
    q_ref, nk_ref, len_ref, cache_ref, res_ref, o_ref, router_ref, gate_ref, up_ref, down_ref, routes_ref,
    att_ref, lay_ref,
    cache_v, o_v, gate_v, up_v, down_v, query_v, mixed_v, heads_v, block_v, lhs_v, wide_v,
    *more,
):
    n, levels, group, width, subs, splits, per_expert, batches = cfg
    more = list(more)

    def take(count):
        return [more.pop(0) for _ in range(count)]

    accs = [take(2) for _ in range(batches)]
    sends = [take(2) for _ in range(batches)]
    landings = [[take(2) for _ in range(2)] for _ in range(batches)]
    rows = [take(2) for _ in range(batches)]
    gates_v = take(batches)
    xs = [take(2) for _ in range(batches)]
    outs = [take(2) for _ in range(batches)]
    cache_sem, load_sem, swap_sem, rs_sem, ag_sem = more
    me = lax.axis_index("req")
    mine = me % group
    orders = [list(range(levels)), list(range(levels))]
    if levels > 2:
        orders[1][1], orders[1][2] = 2, 1
    starts = (0, splits[0])
    rank = levels
    own_place = (0,) * rank
    turns = subs // 2

    def cache_copy(m, k):
        return pltpu.make_async_copy(
            cache_ref.at[m, pl.ds(k * 16, 16)], cache_v.at[m, pl.ds(k * 16, 16)], cache_sem.at[m, k]
        )

    loads = [
        pltpu.make_async_copy(src, dst, load_sem.at[i])
        for i, (src, dst) in enumerate(
            ((o_ref, o_v), (gate_ref, gate_v), (up_ref, up_v), (down_ref, down_v))
        )
    ]
    for m in range(batches):
        for k in range(turns):
            cache_copy(m, k).start()
        if m == 0:
            loads[0].start()

    masks = sorted({1 << d for d in range(levels)} | set(range(1, group)))
    barrier = pltpu.get_barrier_semaphore()
    for mask in masks:
        pl.semaphore_signal(barrier, inc=1, device_id={"req": flip(me, mask)}, device_id_type=MESH)

    factor = 1.0 / math.sqrt(HD)
    lane = lax.broadcasted_iota(jnp.int32, (16, LANES), 1)
    position = lax.broadcasted_iota(jnp.int32, (8, LANES), 1)
    first = mine * subs * 8

    def attend(m, k):
        cache_copy(m, k).wait()
        base = k * 16
        here = pl.ds(pl.multiple_of(base, 16), 16)
        fresh = nk_ref[m, here, :].astype(jnp.float32)
        fresh = jnp.broadcast_to(fresh[:, None, :], (16, 8, LANES)).reshape(128, LANES)
        for j in range(4):
            pair = q_ref[m, here, j * LANES : (j + 1) * LANES].astype(jnp.float32)
            query_v[pl.ds(2 * j, 16, stride=8), :] = jnp.where(lane < HD, pair, 0.0)
            query_v[pl.ds(2 * j + 1, 16, stride=8), :] = jnp.where(lane < HD, pltpu.roll(pair, HD, 1), 0.0)
        masked = []
        for r in range(16):
            score = dot_t(query_v[r * 8 : r * 8 + 8, :].astype(jnp.bfloat16), cache_v[m, base + r])
            live = position < len_ref[m, first + base + r]
            masked.append(jnp.where(live, score * factor, -jnp.inf))
        masked = jnp.concatenate(masked, axis=0)
        own = jnp.sum(query_v[...] * fresh, axis=1, keepdims=True) * factor
        top = jnp.maximum(jnp.max(masked, axis=1, keepdims=True), own)
        weight = jnp.exp(masked - top)
        weight_own = jnp.exp(own - top)
        total = jnp.sum(weight, axis=1, keepdims=True) + weight_own
        probs = weight / total
        prob_own = (weight_own / total).astype(jnp.bfloat16).astype(jnp.float32)
        mixed = []
        for r in range(16):
            mixed.append(
                jnp.dot(
                    probs[r * 8 : r * 8 + 8].astype(jnp.bfloat16),
                    cache_v[m, base + r],
                    preferred_element_type=jnp.float32,
                )
            )
        mixed_v[...] = jnp.concatenate(mixed, axis=0) + prob_own * fresh
        head = [mixed_v[pl.ds(h, 16, stride=8), :] for h in range(8)]
        if width >= LANES:
            for j in range(4):
                pair = jnp.where(lane < HD, pltpu.roll(head[2 * j], HD, 1), head[2 * j + 1])
                dest, col = j * LANES // width, j * LANES % width
                for b in range(2):
                    heads_v[dest, m, 2 * k + b, :, col : col + LANES] = pair[b * 8 : b * 8 + 8]
        else:
            for h in range(8):
                one = pltpu.roll(head[h], HD, 1)[:, :HD]
                for b in range(2):
                    heads_v[h, m, 2 * k + b] = one[b * 8 : b * 8 + 8]

    def attend_range(m, low, high):
        def body(k, carry):
            attend(m, k)
            return carry

        lax.fori_loop(low, high, body, 0)

    def region(order, level, bit):
        index = [slice(None)] * rank
        for d in order[:level]:
            index[d] = 0
        index[order[level]] = bit
        return tuple(index)

    def scatter_step(m, phase, level, copies):
        for c in range(2):
            order, acc, landing = orders[c], accs[m][c], landings[m][phase][c]
            if level:
                copies[level - 1, c].wait_recv()
                done = region(order, level - 1, 1)
                kept = region(order, level - 1, 0)
                acc[kept] = acc[kept] + landing[done].astype(jnp.float32)
            out = region(order, level, 1)
            sends[m][c][out] = acc[out].astype(jnp.bfloat16)
            copies[level, c] = pltpu.make_async_remote_copy(
                src_ref=sends[m][c].at[out],
                dst_ref=landing.at[out],
                send_sem=rs_sem.at[m, phase, 0, level, c],
                recv_sem=rs_sem.at[m, phase, 1, level, c],
                device_id={"req": flip(me, 1 << order[level])},
                device_id_type=MESH,
            )
            copies[level, c].start()

    def scatter_end(m, phase, copies):
        total = []
        for c in range(2):
            copies[levels - 1, c].wait_recv()
            last = region(orders[c], levels - 1, 1)
            kept = region(orders[c], levels - 1, 0)
            total.append(accs[m][c][kept] + landings[m][phase][c][last].astype(jnp.float32))
        for copy in copies.values():
            copy.wait_send()
        return total

    def norm_rows(m, summed):
        square = jnp.zeros((8, 1), jnp.float32)
        attended = []
        for c in range(2):
            cols = slice(starts[c], starts[c] + splits[c])
            value = (res_ref[m, :, cols].astype(jnp.float32) + summed[c]).astype(jnp.bfloat16)
            att_ref[m, :, cols] = value
            value = value.astype(jnp.float32)
            wide_v[m, :, cols] = value
            attended.append(value)
            square = square + jnp.sum(value * value, axis=1, keepdims=True)
        scale = lax.rsqrt(square / (splits[0] + splits[1]) + EPS)
        logits = 0.0
        for c in range(2):
            normed = (attended[c] * scale).astype(jnp.bfloat16)
            rows[m][c][own_place] = normed
            logits = logits + dot_t(normed, router_ref[:, starts[c] : starts[c] + splits[c]])
        experts = router_ref.shape[0]
        ids = lax.broadcasted_iota(jnp.int32, (8, experts), 1).astype(jnp.float32)
        row = lax.broadcasted_iota(jnp.int32, (8, 8), 0)
        col = lax.broadcasted_iota(jnp.int32, (8, 8), 1)
        pick = jnp.where(row == col, 1.0, 0.0).astype(jnp.bfloat16)
        routes = dot_t(pick, routes_ref[m].astype(jnp.float32).astype(jnp.bfloat16))
        named = jnp.zeros((8, experts), jnp.float32)
        for t in range(routes_ref.shape[1]):
            named = jnp.where(ids == routes[:, t : t + 1], 1.0, named)
        live = jnp.where(named > 0.0, logits, -jnp.inf)
        power = jnp.exp(live - jnp.max(live, axis=1, keepdims=True))
        gates = power / jnp.sum(power, axis=1, keepdims=True)
        gates_v[m][own_place] = jnp.concatenate([gates, jnp.zeros((8, LANES - experts), jnp.float32)], axis=1)

    def gather_step(m, level, copies):
        streams = ((rows[m][0], orders[0]), (rows[m][1], orders[1]), (gates_v[m], orders[0]))
        for c, (ref, order) in enumerate(streams):
            if level < levels - 1:
                copies[level + 1, c].wait_recv()
            copies[level, c] = pltpu.make_async_remote_copy(
                src_ref=ref.at[region(order, level, 0)],
                dst_ref=ref.at[region(order, level, 1)],
                send_sem=ag_sem.at[m, 0, level, c],
                recv_sem=ag_sem.at[m, 1, level, c],
                device_id={"req": flip(me, 1 << order[level])},
                device_id_type=MESH,
            )
            copies[level, c].start()

    entries = gate_ref.shape[0]
    expert = me * entries // per_expert
    tiles = n // 16
    tile_bits = tiles.bit_length() - 1

    def expert_entry(m, tile, j):
        lead = tuple((tile >> (tile_bits - 1 - b)) & 1 for b in range(tile_bits))
        at = lead + (slice(None),) * (rank - tile_bits)
        if j == 0:
            for c in range(2):
                wide = rows[m][c][at].astype(jnp.float32).reshape(128, splits[c])
                xs[m][c][...] = wide.astype(jnp.bfloat16)
        hidden = []
        for weights in (gate_v, up_v):
            value = 0.0
            for c in range(2):
                value = value + dot_t(xs[m][c][...], weights[j, :, starts[c] : starts[c] + splits[c]])
            hidden.append(value)
        g, u = hidden
        active = ((u + 1.0) * g * jax.nn.sigmoid(1.702 * g)).astype(jnp.bfloat16)
        for c in range(2):
            part = jnp.dot(
                active, down_v[j, :, starts[c] : starts[c] + splits[c]], preferred_element_type=jnp.float32
            )
            if j:
                part = outs[m][c][...] + part
            if j < entries - 1:
                outs[m][c][...] = part
                continue
            wide_gates = gates_v[m][at].reshape(128, LANES)
            column = lax.broadcasted_iota(jnp.int32, (128, LANES), 1)
            gate = jnp.sum(jnp.where(column == expert, wide_gates, 0.0), axis=1, keepdims=True)
            part = jnp.where(gate > 0.0, part * gate, 0.0)
            accs[m][c][at] = part.reshape((2,) * (rank - tile_bits) + (8, splits[c]))

    group_bits = group.bit_length() - 1
    half = turns // 2

    def chain(m):
        attend_range(m, 0, half)
        yield "attention"
        attend_range(m, half, turns)
        if m == 0:
            for load in loads[1:]:
                load.start()
            pl.semaphore_wait(barrier, len(masks))
        swaps = []
        for j in range(1, group):
            partner = flip(me, j)
            swap = pltpu.make_async_remote_copy(
                src_ref=heads_v.at[partner % group, m],
                dst_ref=block_v.at[j, m],
                send_sem=swap_sem.at[m, 0, j],
                recv_sem=swap_sem.at[m, 1, j],
                device_id={"req": partner},
                device_id_type=MESH,
            )
            swap.start()
            swaps.append(swap)
        block_v[0, m] = heads_v[mine, m]
        yield "swap"
        for swap in swaps:
            swap.wait()
        if m == 0:
            loads[0].wait()
        for place in range(n):
            mask = sum(((place >> (levels - 1 - d)) & 1) << d for d in range(levels))
            dest = flip(me, mask)
            slot = exclusive(dest // subs % group, mine, group_bits)
            lhs_v[m, place] = block_v[slot, m, dest % subs]
        lhs = lhs_v[m].reshape(n * 8, width).astype(jnp.bfloat16)
        for c in range(2):
            part = dot_t(lhs, o_v[starts[c] : starts[c] + splits[c], :])
            accs[m][c][...] = part.reshape(accs[m][c].shape)
        copies = {}
        for level in range(levels):
            scatter_step(m, 0, level, copies)
            yield "reduce"
        norm_rows(m, scatter_end(m, 0, copies))
        copies = {}
        for level in reversed(range(levels)):
            gather_step(m, level, copies)
            yield "gather"
        for c in range(3):
            copies[0, c].wait_recv()
        for copy in copies.values():
            copy.wait_send()
        if m == 0:
            for load in loads[1:]:
                load.wait()
        copies = {}
        for tile in range(tiles):
            for j in range(entries):
                expert_entry(m, tile, j)
                if (tile, j) == (tiles - 1, entries - 1):
                    scatter_step(m, 1, 0, copies)
                yield "expert"
        for level in range(1, levels):
            scatter_step(m, 1, level, copies)
            yield "combine"
        mixture = scatter_end(m, 1, copies)
        for c in range(2):
            cols = slice(starts[c], starts[c] + splits[c])
            lay_ref[m, :, cols] = (wide_v[m, :, cols] + mixture[c]).astype(jnp.bfloat16)
        yield "end"

    units = tiles * entries
    order = [0, 0, 0, 1, 0, 1, 0, 1]
    order += [0, 1] * (levels - 3)
    order += [0, 1] * levels
    order += [0, 1] + [0] * (units // 2) + [1] + [0] * (units - 1 - units // 2) + [1, 0] * levels
    length = 2 + levels + levels + units + levels - 1 + 1
    chains = [chain(m) for m in range(batches)]
    taken = [0] * batches
    for m in order + [0] * length + [1] * length:
        if taken[m] < length:
            next(chains[m])
            taken[m] += 1


def shards(queries, new_kv, cache, lengths, residual, o_proj, router, w_gate, w_up, w_down, routes):
    n = lax.axis_size("req")
    levels = n.bit_length() - 1
    batches, local, q_cols = queries.shape
    depth = residual.shape[2]
    own_rows = residual.shape[1]
    width = o_proj.shape[0]
    group = q_cols // width
    subs = local // own_rows
    heads = q_cols // HD
    per_expert = max(1, n * w_gate.shape[0] // router.shape[1])
    cut = (depth // 2 + LANES - 1) // LANES * LANES
    splits = (cut, depth - cut)

    gate_t, up_t = jnp.swapaxes(w_gate, 1, 2), jnp.swapaxes(w_up, 1, 2)
    cube = (2,) * levels
    f32, b16 = jnp.float32, jnp.bfloat16
    vmem = pl.BlockSpec(memory_space=pltpu.VMEM)
    smem = pl.BlockSpec(memory_space=pltpu.SMEM)
    hbm = pl.BlockSpec(memory_space=pl.ANY)

    def pair(dtype):
        return [pltpu.VMEM(cube + (own_rows, s), dtype) for s in splits]

    scratch = [
        pltpu.VMEM(cache.shape, b16),
        pltpu.VMEM(o_proj.shape[::-1], b16),
        pltpu.VMEM(gate_t.shape, b16),
        pltpu.VMEM(up_t.shape, b16),
        pltpu.VMEM(w_down.shape, b16),
        pltpu.VMEM((16 * heads, LANES), f32),
        pltpu.VMEM((16 * heads, LANES), f32),
        pltpu.VMEM((group, batches, subs, own_rows, width), f32),
        pltpu.VMEM((group, batches, subs, own_rows, width), f32),
        pltpu.VMEM((batches, n, own_rows, width), f32),
        pltpu.VMEM((batches, own_rows, depth), f32),
        *(pair(f32) * batches),
        *(pair(b16) * batches),
        *(pair(b16) * (2 * batches)),
        *(pair(b16) * batches),
        *([pltpu.VMEM(cube + (own_rows, LANES), f32)] * batches),
        *([pltpu.VMEM((128, s), b16) for s in splits] * batches),
        *([pltpu.VMEM((128, s), f32) for s in splits] * batches),
        pltpu.SemaphoreType.DMA((batches, subs // 2)),
        pltpu.SemaphoreType.DMA((4,)),
        pltpu.SemaphoreType.DMA((batches, 2, group)),
        pltpu.SemaphoreType.DMA((batches, 2, 2, levels, 2)),
        pltpu.SemaphoreType.DMA((batches, 2, levels, 3)),
    ]
    out = jax.ShapeDtypeStruct(residual.shape, b16)
    return pl.pallas_call(
        functools.partial(layer_kernel, (n, levels, group, width, subs, splits, per_expert, batches)),
        out_shape=(out, out),
        in_specs=[vmem, vmem, smem, hbm, vmem, hbm, vmem, hbm, hbm, hbm, vmem],
        out_specs=(vmem, vmem),
        scratch_shapes=scratch,
        compiler_params=pltpu.CompilerParams(
            collective_id=0, has_side_effects=True, vmem_limit_bytes=67043328
        ),
        name="moe_layer",
    )(
        queries, new_kv, lengths, cache, residual, o_proj.T, router.T, gate_t, up_t, w_down,
        jnp.swapaxes(routes, 1, 2),
    )


def solution(mesh):
    placed = (
        P(None, ("groups", "req"), None),
        P(None, ("groups", "req"), None),
        P(None, ("groups", "req"), None, None),
        P(None, "groups"),
        P(None, ("groups", "req"), None),
        P("req", None),
        P(),
        P("req", None, None),
        P("req", None, None),
        P("req", None, None),
        P(None, ("groups", "req"), None),
    )
    if tuple(mesh.axis_names) != ("groups", "req"):
        raise ValueError("mesh axes")
    return jax.shard_map(
        shards,
        mesh=mesh,
        in_specs=placed,
        out_specs=(P(None, ("groups", "req"), None), P(None, ("groups", "req"), None)),
        check_vma=False,
    )
```

```python
import functools
import math

import jax
import jax.numpy as jnp
from jax import lax
from jax.experimental import pallas as pl
from jax.experimental.pallas import tpu as pltpu
from jax.sharding import PartitionSpec as P

HD = 64
LANES = 128
EPS = 1e-05
MESH = pl.DeviceIdType.MESH


def flip(value, mask):
    bit = 1
    result = value
    while bit <= mask:
        if mask & bit:
            result = result + bit - 2 * bit * ((value // bit) % 2)
        bit *= 2
    return result


def exclusive(left, right, bits):
    result = left * 0
    for b in range(bits):
        x = (left // (1 << b)) % 2
        y = (right // (1 << b)) % 2
        result = result + (x + y - 2 * x * y) * (1 << b)
    return result


def dot_t(left, right):
    return lax.dot_general(left, right, (((1,), (1,)), ((), ())), preferred_element_type=jnp.float32)


def layer_kernel(
    cfg,
    q_ref, nk_ref, len_ref, cache_ref, res_ref, o_ref, router_ref, gate_ref, up_ref, down_ref, routes_ref,
    att_ref, lay_ref,
    cache_v, o_v, gate_v, up_v, down_v, query_v, mixed_v, heads_v, block_v, lhs_v, wide_v,
    *more,
):
    n, levels, group, width, subs, splits, per_expert, batches = cfg
    more = list(more)

    def take(count):
        return [more.pop(0) for _ in range(count)]

    accs = [take(2) for _ in range(batches)]
    sends = [take(2) for _ in range(batches)]
    landings = [[take(2) for _ in range(2)] for _ in range(batches)]
    rows = [take(2) for _ in range(batches)]
    gates_v = take(batches)
    xs = [take(2) for _ in range(batches)]
    outs = [take(2) for _ in range(batches)]
    cache_sem, load_sem, swap_sem, rs_sem, ag_sem = more
    me = lax.axis_index("req")
    mine = me % group
    orders = [list(range(levels)), list(range(levels))]
    if levels > 2:
        orders[1][1], orders[1][2] = 2, 1
    starts = (0, splits[0])
    rank = levels
    own_place = (0,) * rank
    turns = subs // 2

    def cache_copy(m, k):
        return pltpu.make_async_copy(
            cache_ref.at[m, pl.ds(k * 16, 16)], cache_v.at[m, pl.ds(k * 16, 16)], cache_sem.at[m, k]
        )

    loads = [
        pltpu.make_async_copy(src, dst, load_sem.at[i])
        for i, (src, dst) in enumerate(
            ((o_ref, o_v), (gate_ref, gate_v), (up_ref, up_v), (down_ref, down_v))
        )
    ]
    for m in range(batches):
        for k in range(turns):
            cache_copy(m, k).start()
        if m == 0:
            loads[0].start()

    masks = sorted({1 << d for d in range(levels)} | set(range(1, group)))
    barrier = pltpu.get_barrier_semaphore()
    for mask in masks:
        pl.semaphore_signal(barrier, inc=1, device_id={"req": flip(me, mask)}, device_id_type=MESH)

    factor = 1.0 / math.sqrt(HD)
    lane = lax.broadcasted_iota(jnp.int32, (16, LANES), 1)
    position = lax.broadcasted_iota(jnp.int32, (8, LANES), 1)
    first = mine * subs * 8

    def attend(m, k):
        cache_copy(m, k).wait()
        base = k * 16
        here = pl.ds(pl.multiple_of(base, 16), 16)
        fresh = nk_ref[m, here, :].astype(jnp.float32)
        fresh = jnp.broadcast_to(fresh[:, None, :], (16, 8, LANES)).reshape(128, LANES)
        for j in range(4):
            pair = q_ref[m, here, j * LANES : (j + 1) * LANES].astype(jnp.float32)
            query_v[pl.ds(2 * j, 16, stride=8), :] = jnp.where(lane < HD, pair, 0.0)
            query_v[pl.ds(2 * j + 1, 16, stride=8), :] = jnp.where(lane < HD, pltpu.roll(pair, HD, 1), 0.0)
        masked = []
        for r in range(16):
            score = dot_t(query_v[r * 8 : r * 8 + 8, :].astype(jnp.bfloat16), cache_v[m, base + r])
            live = position < len_ref[m, first + base + r]
            masked.append(jnp.where(live, score * factor, -jnp.inf))
        masked = jnp.concatenate(masked, axis=0)
        own = jnp.sum(query_v[...] * fresh, axis=1, keepdims=True) * factor
        top = jnp.maximum(jnp.max(masked, axis=1, keepdims=True), own)
        weight = jnp.exp(masked - top)
        weight_own = jnp.exp(own - top)
        total = jnp.sum(weight, axis=1, keepdims=True) + weight_own
        probs = weight / total
        prob_own = (weight_own / total).astype(jnp.bfloat16).astype(jnp.float32)
        mixed = []
        for r in range(16):
            mixed.append(
                jnp.dot(
                    probs[r * 8 : r * 8 + 8].astype(jnp.bfloat16),
                    cache_v[m, base + r],
                    preferred_element_type=jnp.float32,
                )
            )
        mixed_v[...] = jnp.concatenate(mixed, axis=0) + prob_own * fresh
        head = [mixed_v[pl.ds(h, 16, stride=8), :] for h in range(8)]
        if width >= LANES:
            for j in range(4):
                pair = jnp.where(lane < HD, pltpu.roll(head[2 * j], HD, 1), head[2 * j + 1])
                dest, col = j * LANES // width, j * LANES % width
                for b in range(2):
                    heads_v[dest, m, 2 * k + b, :, col : col + LANES] = pair[b * 8 : b * 8 + 8]
        else:
            for h in range(8):
                one = pltpu.roll(head[h], HD, 1)[:, :HD]
                for b in range(2):
                    heads_v[h, m, 2 * k + b] = one[b * 8 : b * 8 + 8]

    def attend_range(m, low, high):
        def body(k, carry):
            attend(m, k)
            return carry

        lax.fori_loop(low, high, body, 0)

    def region(order, level, bit):
        index = [slice(None)] * rank
        for d in order[:level]:
            index[d] = 0
        index[order[level]] = bit
        return tuple(index)

    def scatter_step(m, phase, level, copies):
        arrived = lambda c, at: tuple(1 if d == orders[c][level - 1] else i for d, i in enumerate(at))
        for c in range(2):
            order, acc, landing = orders[c], accs[m][c], landings[m][phase][c]
            out = region(order, level, 1)
            value = acc[out]
            if level:
                copies[level - 1, c].wait_recv()
                value = value + landing[arrived(c, out)].astype(jnp.float32)
            sends[m][c][out] = value.astype(jnp.bfloat16)
            copies[level, c] = pltpu.make_async_remote_copy(
                src_ref=sends[m][c].at[out],
                dst_ref=landing.at[out],
                send_sem=rs_sem.at[m, phase, 0, level, c],
                recv_sem=rs_sem.at[m, phase, 1, level, c],
                device_id={"req": flip(me, 1 << order[level])},
                device_id_type=MESH,
            )
            copies[level, c].start()
        if level:
            for c in range(2):
                kept = region(orders[c], level, 0)
                value = landings[m][phase][c][arrived(c, kept)].astype(jnp.float32)
                accs[m][c][kept] = accs[m][c][kept] + value

    def scatter_end(m, phase, copies):
        total = []
        for c in range(2):
            copies[levels - 1, c].wait_recv()
            last = region(orders[c], levels - 1, 1)
            kept = region(orders[c], levels - 1, 0)
            total.append(accs[m][c][kept] + landings[m][phase][c][last].astype(jnp.float32))
        for copy in copies.values():
            copy.wait_send()
        return total

    def norm_rows(m, summed):
        square = jnp.zeros((8, 1), jnp.float32)
        attended = []
        for c in range(2):
            cols = slice(starts[c], starts[c] + splits[c])
            value = (res_ref[m, :, cols].astype(jnp.float32) + summed[c]).astype(jnp.bfloat16)
            att_ref[m, :, cols] = value
            value = value.astype(jnp.float32)
            wide_v[m, :, cols] = value
            attended.append(value)
            square = square + jnp.sum(value * value, axis=1, keepdims=True)
        scale = lax.rsqrt(square / (splits[0] + splits[1]) + EPS)
        logits = 0.0
        for c in range(2):
            normed = (attended[c] * scale).astype(jnp.bfloat16)
            rows[m][c][own_place] = normed
            logits = logits + dot_t(normed, router_ref[:, starts[c] : starts[c] + splits[c]])
        experts = router_ref.shape[0]
        ids = lax.broadcasted_iota(jnp.int32, (8, experts), 1).astype(jnp.float32)
        row = lax.broadcasted_iota(jnp.int32, (8, 8), 0)
        col = lax.broadcasted_iota(jnp.int32, (8, 8), 1)
        pick = jnp.where(row == col, 1.0, 0.0).astype(jnp.bfloat16)
        routes = dot_t(pick, routes_ref[m].astype(jnp.float32).astype(jnp.bfloat16))
        named = jnp.zeros((8, experts), jnp.float32)
        for t in range(routes_ref.shape[1]):
            named = jnp.where(ids == routes[:, t : t + 1], 1.0, named)
        live = jnp.where(named > 0.0, logits, -jnp.inf)
        power = jnp.exp(live - jnp.max(live, axis=1, keepdims=True))
        gates = power / jnp.sum(power, axis=1, keepdims=True)
        gates_v[m][own_place] = jnp.concatenate([gates, jnp.zeros((8, LANES - experts), jnp.float32)], axis=1)

    def gather_step(m, level, copies):
        streams = ((rows[m][0], orders[0]), (rows[m][1], orders[1]), (gates_v[m], orders[0]))
        for c, (ref, order) in enumerate(streams):
            if level < levels - 1:
                copies[level + 1, c].wait_recv()
            copies[level, c] = pltpu.make_async_remote_copy(
                src_ref=ref.at[region(order, level, 0)],
                dst_ref=ref.at[region(order, level, 1)],
                send_sem=ag_sem.at[m, 0, level, c],
                recv_sem=ag_sem.at[m, 1, level, c],
                device_id={"req": flip(me, 1 << order[level])},
                device_id_type=MESH,
            )
            copies[level, c].start()

    entries = gate_ref.shape[0]
    expert = me * entries // per_expert
    tiles = n // 16
    tile_bits = tiles.bit_length() - 1

    def expert_entry(m, tile, j):
        lead = tuple((tile >> (tile_bits - 1 - b)) & 1 for b in range(tile_bits))
        at = lead + (slice(None),) * (rank - tile_bits)
        if j == 0:
            for c in range(2):
                wide = rows[m][c][at].astype(jnp.float32).reshape(128, splits[c])
                xs[m][c][...] = wide.astype(jnp.bfloat16)
        hidden = []
        for weights in (gate_v, up_v):
            value = 0.0
            for c in range(2):
                value = value + dot_t(xs[m][c][...], weights[j, :, starts[c] : starts[c] + splits[c]])
            hidden.append(value)
        g, u = hidden
        active = ((u + 1.0) * g * jax.nn.sigmoid(1.702 * g)).astype(jnp.bfloat16)
        for c in range(2):
            part = jnp.dot(
                active, down_v[j, :, starts[c] : starts[c] + splits[c]], preferred_element_type=jnp.float32
            )
            if j:
                part = outs[m][c][...] + part
            if j < entries - 1:
                outs[m][c][...] = part
                continue
            wide_gates = gates_v[m][at].reshape(128, LANES)
            column = lax.broadcasted_iota(jnp.int32, (128, LANES), 1)
            gate = jnp.sum(jnp.where(column == expert, wide_gates, 0.0), axis=1, keepdims=True)
            part = jnp.where(gate > 0.0, part * gate, 0.0)
            accs[m][c][at] = part.reshape((2,) * (rank - tile_bits) + (8, splits[c]))

    group_bits = group.bit_length() - 1
    half = turns // 2

    def chain(m):
        attend_range(m, 0, half)
        yield "attention"
        attend_range(m, half, turns)
        if m == 0:
            for load in loads[1:]:
                load.start()
            pl.semaphore_wait(barrier, len(masks))
        swaps = []
        for j in range(1, group):
            partner = flip(me, j)
            swap = pltpu.make_async_remote_copy(
                src_ref=heads_v.at[partner % group, m],
                dst_ref=block_v.at[j, m],
                send_sem=swap_sem.at[m, 0, j],
                recv_sem=swap_sem.at[m, 1, j],
                device_id={"req": partner},
                device_id_type=MESH,
            )
            swap.start()
            swaps.append(swap)
        block_v[0, m] = heads_v[mine, m]
        yield "swap"
        for swap in swaps:
            swap.wait()
        if m == 0:
            loads[0].wait()
        for place in range(n):
            mask = sum(((place >> (levels - 1 - d)) & 1) << d for d in range(levels))
            dest = flip(me, mask)
            slot = exclusive(dest // subs % group, mine, group_bits)
            lhs_v[m, place] = block_v[slot, m, dest % subs]
        lhs = lhs_v[m].reshape(n * 8, width).astype(jnp.bfloat16)
        for c in range(2):
            part = dot_t(lhs, o_v[starts[c] : starts[c] + splits[c], :])
            accs[m][c][...] = part.reshape(accs[m][c].shape)
        copies = {}
        for level in range(levels):
            scatter_step(m, 0, level, copies)
            yield "reduce"
        norm_rows(m, scatter_end(m, 0, copies))
        copies = {}
        for level in reversed(range(levels)):
            gather_step(m, level, copies)
            yield "gather"
        for c in range(3):
            copies[0, c].wait_recv()
        for copy in copies.values():
            copy.wait_send()
        if m == 0:
            for load in loads[1:]:
                load.wait()
        copies = {}
        for tile in range(tiles):
            for j in range(entries):
                expert_entry(m, tile, j)
                if (tile, j) == (tiles - 1, entries - 1):
                    scatter_step(m, 1, 0, copies)
                yield "expert"
        for level in range(1, levels):
            scatter_step(m, 1, level, copies)
            yield "combine"
        mixture = scatter_end(m, 1, copies)
        for c in range(2):
            cols = slice(starts[c], starts[c] + splits[c])
            lay_ref[m, :, cols] = (wide_v[m, :, cols] + mixture[c]).astype(jnp.bfloat16)
        yield "end"

    units = tiles * entries
    order = [0, 0, 0, 1, 0, 1, 0, 1]
    order += [0, 1] * (levels - 3)
    order += [0, 1] * levels
    order += [0, 1] + [0] * (units // 2) + [1] + [0] * (units - 1 - units // 2) + [1, 0] * levels
    length = 2 + levels + levels + units + levels - 1 + 1
    chains = [chain(m) for m in range(batches)]
    taken = [0] * batches
    for m in order + [0] * length + [1] * length:
        if taken[m] < length:
            next(chains[m])
            taken[m] += 1


def shards(queries, new_kv, cache, lengths, residual, o_proj, router, w_gate, w_up, w_down, routes):
    n = lax.axis_size("req")
    levels = n.bit_length() - 1
    batches, local, q_cols = queries.shape
    depth = residual.shape[2]
    own_rows = residual.shape[1]
    width = o_proj.shape[0]
    group = q_cols // width
    subs = local // own_rows
    heads = q_cols // HD
    per_expert = max(1, n * w_gate.shape[0] // router.shape[1])
    cut = (depth // 2 + LANES - 1) // LANES * LANES
    splits = (cut, depth - cut)

    gate_t, up_t = jnp.swapaxes(w_gate, 1, 2), jnp.swapaxes(w_up, 1, 2)
    cube = (2,) * levels
    f32, b16 = jnp.float32, jnp.bfloat16
    vmem = pl.BlockSpec(memory_space=pltpu.VMEM)
    smem = pl.BlockSpec(memory_space=pltpu.SMEM)
    hbm = pl.BlockSpec(memory_space=pl.ANY)

    def pair(dtype):
        return [pltpu.VMEM(cube + (own_rows, s), dtype) for s in splits]

    scratch = [
        pltpu.VMEM(cache.shape, b16),
        pltpu.VMEM(o_proj.shape[::-1], b16),
        pltpu.VMEM(gate_t.shape, b16),
        pltpu.VMEM(up_t.shape, b16),
        pltpu.VMEM(w_down.shape, b16),
        pltpu.VMEM((16 * heads, LANES), f32),
        pltpu.VMEM((16 * heads, LANES), f32),
        pltpu.VMEM((group, batches, subs, own_rows, width), f32),
        pltpu.VMEM((group, batches, subs, own_rows, width), f32),
        pltpu.VMEM((batches, n, own_rows, width), f32),
        pltpu.VMEM((batches, own_rows, depth), f32),
        *(pair(f32) * batches),
        *(pair(b16) * batches),
        *(pair(b16) * (2 * batches)),
        *(pair(b16) * batches),
        *([pltpu.VMEM(cube + (own_rows, LANES), f32)] * batches),
        *([pltpu.VMEM((128, s), b16) for s in splits] * batches),
        *([pltpu.VMEM((128, s), f32) for s in splits] * batches),
        pltpu.SemaphoreType.DMA((batches, subs // 2)),
        pltpu.SemaphoreType.DMA((4,)),
        pltpu.SemaphoreType.DMA((batches, 2, group)),
        pltpu.SemaphoreType.DMA((batches, 2, 2, levels, 2)),
        pltpu.SemaphoreType.DMA((batches, 2, levels, 3)),
    ]
    out = jax.ShapeDtypeStruct(residual.shape, b16)
    return pl.pallas_call(
        functools.partial(layer_kernel, (n, levels, group, width, subs, splits, per_expert, batches)),
        out_shape=(out, out),
        in_specs=[vmem, vmem, smem, hbm, vmem, hbm, vmem, hbm, hbm, hbm, vmem],
        out_specs=(vmem, vmem),
        scratch_shapes=scratch,
        compiler_params=pltpu.CompilerParams(
            collective_id=0, has_side_effects=True, vmem_limit_bytes=67043328
        ),
        name="moe_layer",
    )(
        queries, new_kv, lengths, cache, residual, o_proj.T, router.T, gate_t, up_t, w_down,
        jnp.swapaxes(routes, 1, 2),
    )


def solution(mesh):
    placed = (
        P(None, ("groups", "req"), None),
        P(None, ("groups", "req"), None),
        P(None, ("groups", "req"), None, None),
        P(None, "groups"),
        P(None, ("groups", "req"), None),
        P("req", None),
        P(),
        P("req", None, None),
        P("req", None, None),
        P("req", None, None),
        P(None, ("groups", "req"), None),
    )
    if tuple(mesh.axis_names) != ("groups", "req"):
        raise ValueError("mesh axes")
    return jax.shard_map(
        shards,
        mesh=mesh,
        in_specs=placed,
        out_specs=(P(None, ("groups", "req"), None), P(None, ("groups", "req"), None)),
        check_vma=False,
    )
```
